256 devices in a mesh: slab: 32 (over y, x, z_lo), blk: 8 (over z_hi, core).
Axes of the slice: x: 4, y: 4, z: 8 (z_hi: 4, z_lo: 2; z = z_hi * 2 + z_lo), core: 2. Of those that a mesh axis runs over, the one named last changes fastest.
Arguments:
- interior: float32 [64, 512, 512], P('slab', 'blk'), may hold values from -6 to 6
- sources: float32 [64, 512, 512], P('slab', 'blk'), may hold values from -12 to 12
- absorption: float32 [64, 512, 512], P('slab', 'blk'), may hold values from 0.1 to 4
- bem_panel: bfloat16 [8192, 131072], P('blk', 'slab'), may hold values from -0.03125 to 0.03125
- incident: bfloat16 [131072, 512], P('slab'), may hold values from -160 to 160
- node_cell: int32 [131072], P('slab'), may hold values from 0 to 255
- offset: int32 [1], replicated, may hold values from 0 to 122880, as said below
Outputs:
- relaxed: float32 [64, 512, 512], P('slab', 'blk')
- boundary_flux: float32 [8192, 512], P(('blk', 'slab'))
The draws below stay inside these ranges and needn't reach their ends.
Inputs may be any that keep to these rules, and one draw needn't show every extreme that they name: offset is a multiple of 8192; rows offset to offset + 8191 lie among the 131072 boundary nodes.
All inputs are finite; a program needn't handle non-finite values.
Results may differ from the reference program's by a relative error of at most 0.0034.
Values sent between devices are 32-bit elements; how exact they have to be, the bound alone decides.
A program may use at most 64 MiB of HBM per device.

```python
import math
import jax
import jax.numpy as jnp
from jax import lax

CZ = 2
CY = 64
NX = 512
C_DEV = 512
PR = 8192
NRHS = 512
SWEEPS = 2
NZ = 64
NY = 512
NB = 131072
N_BLK = 8


def draw_incident(key, part):
    key_base, key_row, key_col = jax.random.split(key, 3)
    position = jnp.arange(NB, dtype=jnp.float32) / NB
    row_scale = 10.0 ** jax.random.uniform(key_row, (NB,), jnp.float32)
    col_scale = 10.0 ** jax.random.uniform(key_col, (NRHS,), jnp.float32)
    ramp = jnp.exp(jnp.log(3.0) * position)
    base = jnp.clip(jax.random.normal(key_base, (NB, NRHS), jnp.float32), -4.0, 4.0)
    values = 0.04 * base * (row_scale * ramp)[:, None] * col_scale[None, :]
    return values.astype(jnp.bfloat16)


def draw_offset(key, part):
    return (jax.random.randint(key, (1,), 0, NB // PR) * PR).astype(jnp.int32)


def touch_ends(result, key, smallest, largest):
    spot = [jax.random.randint(jax.random.fold_in(key, axis), (), 0, length) for axis, length in enumerate(result.shape)]
    main_axis = result.shape.index(max(result.shape))
    neighbour = spot[:main_axis] + [(spot[main_axis] + 1) % result.shape[main_axis]] + spot[main_axis + 1:]
    return result.at[tuple(spot)].set(smallest).at[tuple(neighbour)].set(largest)


def raised(values, key, source, target, blocks, factor):
    owner, partner = [(jnp.arange(values.shape[dim]) // (values.shape[dim] // blocks)).reshape([-1 if axis == dim else 1 for axis in range(values.ndim)]) for dim in (source, target)]
    chosen = jax.random.permutation(key, blocks)[partner]
    strong = (owner == chosen) | (owner == (partner + blocks // 2) % blocks)
    return jnp.where(strong, factor * values, values)


def block_scale(key, shape, pieces, least, largest):
    loudness, own = 1.0, jax.random.fold_in(key, 6)
    for dim, parts in pieces:
        heights = jnp.exp(jax.random.uniform(jax.random.fold_in(own, dim), (parts,), jnp.float32, least / len(pieces), largest / len(pieces)))
        loudness = loudness * jnp.repeat(heights, shape[dim] // parts).reshape([-1 if axis == dim else 1 for axis in range(len(shape))])
    return loudness


def gaussian(rng, shape, width, reach, cuts=(), held_as=jnp.bfloat16):
    entries = width * jax.random.normal(rng, shape, jnp.float32)
    if cuts:
        entries = entries * block_scale(rng, shape, cuts, -0.22, 0.18)
    return jnp.clip(entries, -reach, reach).astype(held_as)


def heavy_noise(key, shape, deviation, reach, cuts, heavy, kind=jnp.bfloat16):
    entries = deviation * jax.random.normal(key, shape, jnp.float32)
    if cuts:
        entries = entries * block_scale(key, shape, cuts, -0.22, 0.18)
    return jnp.clip(raised(entries, jax.random.fold_in(key, 3), *heavy), -reach, reach).astype(kind)


def setup_inputs(seed: int = 0) -> dict:
    key_list = jax.random.split(jax.random.key(seed), 8)
    return {
        "interior": gaussian(key_list[0], (NZ, NY, NX), 1.0, 6.0, ((0, 32), (1, 8)), jnp.float32),
        "sources": gaussian(key_list[1], (NZ, NY, NX), 2.0, 12.0, ((0, 32), (1, 8)), jnp.float32),
        "absorption": jnp.clip(jnp.exp(math.log(4.0) - 3.6888794 * jax.random.uniform(key_list[2], (NZ, NY, NX), jnp.float32) ** block_scale(key_list[2], (NZ, NY, NX), ((0, 32), (1, 8)), -0.2, 0.2)), 0.1, 4.0),
        "bem_panel": heavy_noise(key_list[3], (PR, NB), NB ** -0.5, 0.03125, ((0, 8), (1, 32)), (1, 0, 32, 2.75)),
        "incident": draw_incident(jax.random.fold_in(key_list[7], 71), 0),
        "node_cell": touch_ends(jax.random.randint(key_list[5], (NB,), 0, 2 * CZ * CY), jax.random.fold_in(key_list[5], 1), 0, (2 * CZ * CY) - 1).astype(jnp.int32),
        "offset": draw_offset(jax.random.fold_in(key_list[7], 71), 0),
    }


omega = 0.6
center_weight = 8.0 / 3.0

def stiffness(padded):
    along_x = padded[:, :, :-2] + padded[:, :, 2:]
    middle = padded[:, :, 1:-1]
    plus_mid = along_x + middle
    plane_sum = plus_mid[:, :-2] + plus_mid[:, 1:-1] + plus_mid[:, 2:]
    total_sum = plane_sum[:-2] + plane_sum[1:-1] + plane_sum[2:]
    cross_xy = along_x[:, :-2] + along_x[:, 2:]
    corner_sum = cross_xy[:-2] + cross_xy[2:]
    face_sum = along_x[1:-1, 1:-1] + middle[1:-1, :-2] + middle[1:-1, 2:] + middle[:-2, 1:-1] + middle[2:, 1:-1]
    center = middle[1:-1, 1:-1]
    edge_sum = total_sum - center - face_sum - corner_sum
    return center_weight * center - edge_sum / 6.0 - corner_sum / 12.0

def sweep_once(padded, sources, absorption):
    center = padded[1:-1, 1:-1, 1:-1]
    applied = stiffness(padded) + absorption * center
    return center + omega * (sources - applied) / (center_weight + absorption)

def reference(interior, sources, absorption, bem_panel, incident, node_cell, offset):
    current = interior
    for sweep_idx in range(SWEEPS):
        current = sweep_once(jnp.pad(current, 1), sources, absorption)
    nodes = jnp.arange(NB, dtype=jnp.int32)
    block = nodes // C_DEV
    zpos = block // N_BLK * CZ + node_cell // (2 * CY)
    ypos = block % N_BLK * CY + node_cell // 2 % CY
    xpos = node_cell % 2 * (NX - 1)
    trace = interior[zpos, ypos, xpos]
    fields = (incident.astype(jnp.float32) + trace[:, None]).astype(jnp.bfloat16)
    wide = fields.astype(jnp.float32)
    norms = jnp.sqrt(lax.optimization_barrier(jnp.sum(wide * wide, axis=0)) / NB + 1e-06)
    jump = lax.dynamic_slice_in_dim(wide, offset[0].astype(jnp.int32), PR, 0)
    product = jnp.dot(bem_panel, fields, preferred_element_type=jnp.float32) + 0.5 * jump
    return (current, product / norms[None, :])
```

```python
import jax
import jax.numpy as jnp
from jax import lax
from jax.experimental import pallas as pl
from jax.experimental.pallas import tpu as pltpu
from jax.sharding import PartitionSpec as P

MESH = pl.DeviceIdType.MESH
F32 = jnp.float32
BF16 = jnp.bfloat16
OMEGA = 0.6
CENTER = 8.0 / 3.0

NSLAB, NBLK = 32, 8
NY, NX, NZ = 4, 4, 2
CHUNKS = 2
OPP, RIGHT, LEFT, OWN = 2, 1, 3, 0


def remote(src, dst, send_sem, recv_sem, device):
    return pltpu.make_async_remote_copy(
        src_ref=src,
        dst_ref=dst,
        send_sem=send_sem,
        recv_sem=recv_sem,
        device_id=device,
        device_id_type=MESH,
    )


def kernel(
    offset_ref,
    interior_ref,
    sources_ref,
    absorption_ref,
    panel_ref,
    incident_ref,
    cells_ref,
    relaxed_ref,
    flux_ref,
    grid0,
    grid1,
    src_v,
    abs_v,
    cells_v,
    inc_v,
    pan_v,
    acc,
    rx1,
    rx2,
    rx3,
    ysend,
    yrecv,
    trace,
    tmat,
    msgs,
    a2a,
    strip_sem,
    load_sem,
    s1_send,
    s1_recv,
    s2_send,
    s2_recv,
    s3_send,
    s3_recv,
    hz_send,
    hz_recv,
    hy_send,
    hy_recv,
    tr_send,
    tr_recv,
    aa_send,
    aa_recv,
):
    s = lax.axis_index("slab")
    b = lax.axis_index("blk")
    py = s // (NX * NZ)
    px = (s // NZ) % NX
    pz = s % NZ
    depth, rows, width = interior_ref.shape
    half = inc_v.shape[2] // 2
    chunk = rows // CHUNKS

    def slab_at(y, x, z):
        return ((y % NY) * NX + x % NX) * NZ + z

    loads = [
        pltpu.make_async_copy(interior_ref, grid0.at[1 : 1 + depth, 8 : 8 + rows, :], load_sem.at[0]),
        pltpu.make_async_copy(cells_ref, cells_v, load_sem.at[1]),
        pltpu.make_async_copy(incident_ref.at[:, :, 0:half], inc_v.at[:, :, 0:half], load_sem.at[2]),
        pltpu.make_async_copy(incident_ref.at[:, :, half:], inc_v.at[:, :, half:], load_sem.at[3]),
        pltpu.make_async_copy(sources_ref, src_v, load_sem.at[4]),
        pltpu.make_async_copy(absorption_ref, abs_v, load_sem.at[5]),
    ]

    def strip(dy, dx):
        yy = (py + dy) % NY
        xx = (px + dx) % NX
        return pltpu.make_async_copy(panel_ref.at[yy, xx], pan_v.at[yy, xx], strip_sem.at[dy, dx])

    order = [(0, OPP), (1, OPP), (0, RIGHT), (0, LEFT), (1, RIGHT), (1, LEFT), (0, OWN), (1, OWN)]

    def strips_of(h, step):
        return [(step, d) for d in range(4)] if h == 0 else [(d, step) for d in range(4)]

    loads[0].start()
    loads[1].start()
    loads[2].start()
    started = set()
    for n, (h, step) in enumerate(order):
        for key in strips_of(h, step):
            if key not in started:
                started.add(key)
                strip(*key).start()
        if n == 0:
            loads[3].start()
    loads[4].start()
    loads[5].start()

    barrier = pltpu.get_barrier_semaphore()

    def greet_slab(k, carry):
        pl.semaphore_signal(barrier, inc=1, device_id=((s + k) % NSLAB, b), device_id_type=MESH)
        return carry

    def greet_blk(k, carry):
        pl.semaphore_signal(barrier, inc=1, device_id=(s, (b + k) % NBLK), device_id_type=MESH)
        return carry

    lax.fori_loop(1, NSLAB, greet_slab, 0)
    lax.fori_loop(1, NBLK, greet_blk, 0)
    for ds in (1, NSLAB - 1):
        for db in (1, NBLK - 1):
            pl.semaphore_signal(
                barrier, inc=1, device_id=((s + ds) % NSLAB, (b + db) % NBLK), device_id_type=MESH
            )

    @pl.when(s == 0)
    def _():
        grid0[0, 8 : 8 + rows, :] = jnp.zeros((rows, width), F32)
        grid1[0, 8 : 8 + rows, :] = jnp.zeros((rows, width), F32)

    @pl.when(s == NSLAB - 1)
    def _():
        grid0[depth + 1, 8 : 8 + rows, :] = jnp.zeros((rows, width), F32)
        grid1[depth + 1, 8 : 8 + rows, :] = jnp.zeros((rows, width), F32)

    loads[0].wait()
    loads[1].wait()

    def pack_rows(grid, rnd, side):
        row = 8 if side == 0 else 7 + rows
        first = grid[1, row : row + 1, :]
        second = grid[2, row : row + 1, :]
        ysend[rnd, side] = jnp.concatenate([first, second, jnp.zeros((6, width), F32)], axis=0)

    pack_rows(grid0, 0, 0)
    pack_rows(grid0, 0, 1)

    low = [grid0[1 + z, 8 : 8 + rows, 0:128][:, 0:1] for z in range(depth)]
    high = [grid0[1 + z, 8 : 8 + rows, width - 128 :][:, 127:128] for z in range(depth)]
    faces = jnp.concatenate(low + high, axis=0)
    count = faces.shape[0]
    position = lax.broadcasted_iota(jnp.int32, (count, 128), 0)
    trace_rows = []
    for q in range(4):
        cell = cells_v[pl.ds(4 * b + q, 1), :]
        code = (cell & 1) * (depth * rows) + (cell // (2 * rows)) * rows + (cell // 2) % rows
        hit = position == code
        trace_rows.append(jnp.sum(jnp.where(hit, faces, 0.0), axis=0, keepdims=True))
    trace[b] = jnp.concatenate(trace_rows + [jnp.zeros((4, 128), F32)], axis=0)

    pl.semaphore_wait(barrier, NSLAB - 1 + NBLK - 1 + 4)

    up = (s + 1) % NSLAB
    down = (s + NSLAB - 1) % NSLAB

    def halo_z(grid, rnd, c, way):
        span = pl.ds(8 + c * chunk, chunk)
        if way == 0:
            return remote(
                grid.at[depth, span], grid.at[0, span], hz_send.at[rnd, c, 0], hz_recv.at[rnd, c, 0], (up, b)
            )
        return remote(
            grid.at[1, span], grid.at[depth + 1, span], hz_send.at[rnd, c, 1], hz_recv.at[rnd, c, 1], (down, b)
        )

    def halo_y(rnd, side, slot):
        target_s = (up, s, down)[slot]
        target_b = (b + NBLK - 1) % NBLK if side == 0 else (b + 1) % NBLK
        return remote(
            ysend.at[rnd, side],
            yrecv.at[rnd, side, slot],
            hy_send.at[rnd, side, slot],
            hy_recv.at[rnd, side, slot],
            (target_s, target_b),
        )

    def start_z(grid, rnd, c):
        @pl.when(s < NSLAB - 1)
        def _():
            halo_z(grid, rnd, c, 0).start()

        @pl.when(s > 0)
        def _():
            halo_z(grid, rnd, c, 1).start()

    def wait_z(grid, rnd, c):
        @pl.when(s > 0)
        def _():
            halo_z(grid, rnd, c, 0).wait_recv()

        @pl.when(s < NSLAB - 1)
        def _():
            halo_z(grid, rnd, c, 1).wait_recv()

    def drain_z(grid, rnd, c):
        @pl.when(s < NSLAB - 1)
        def _():
            halo_z(grid, rnd, c, 0).wait_send()

        @pl.when(s > 0)
        def _():
            halo_z(grid, rnd, c, 1).wait_send()

    def start_y(rnd, side):
        for slot in range(3):
            halo_y(rnd, side, slot).start()

    has_down = jnp.where(s > 0, 1.0, 0.0).astype(F32)
    has_up = jnp.where(s < NSLAB - 1, 1.0, 0.0).astype(F32)
    has_left = jnp.where(b > 0, 1.0, 0.0).astype(F32)
    has_right = jnp.where(b < NBLK - 1, 1.0, 0.0).astype(F32)

    def place_y(grid, rnd, edge):
        side = 1 - edge
        for slot in range(3):
            halo_y(rnd, side, slot).wait_recv()
        there = has_left if edge == 0 else has_right
        row = 7 if edge == 0 else 8 + rows
        grid[0, row : row + 1, :] = yrecv[rnd, side, 0, 1:2, :] * (there * has_down)
        grid[1, row : row + 1, :] = yrecv[rnd, side, 1, 0:1, :] * there
        grid[2, row : row + 1, :] = yrecv[rnd, side, 1, 1:2, :] * there
        grid[3, row : row + 1, :] = yrecv[rnd, side, 2, 0:1, :] * (there * has_up)

    def copy_trace(k):
        return remote(trace.at[b], trace.at[b], tr_send.at[k], tr_recv.at[k], (s, (b + k) % NBLK))

    def landed_trace(k):
        other = (b + NBLK - k) % NBLK
        return remote(trace.at[other], trace.at[other], tr_send.at[k], tr_recv.at[k], (s, other))

    for c in range(CHUNKS):
        start_z(grid0, 0, c)
    for k in range(1, NBLK):
        copy_trace(k).start()
    start_y(0, 0)
    start_y(0, 1)

    weight = jnp.where(2 * (offset_ref[0] // (2 * NBLK * 512)) + b // 4 == s, 0.5, 0.0).astype(F32)
    first = (py, px)
    second = (px, py)

    def at1(h, step):
        return (first[h] + step) % 4

    def at2(h, step):
        return (second[h] + step) % 4

    def dev1(h, step):
        if h == 0:
            return (slab_at(py + step, px, pz), b)
        return (slab_at(py, px + step, pz), b)

    def dev2(h, step):
        return dev1(1 - h, step)

    def stage1(h, kind):
        src, step = {
            0: (acc.at[h, at1(h, OPP), 0:2], RIGHT),
            1: (acc.at[h, at1(h, RIGHT), 2:4], RIGHT),
            2: (acc.at[h, at1(h, OPP), 2:4], LEFT),
            3: (acc.at[h, at1(h, LEFT), 0:2], LEFT),
            4: (acc.at[h, at1(h, RIGHT), 0:2], RIGHT),
            5: (acc.at[h, at1(h, LEFT), 2:4], LEFT),
        }[kind]
        return remote(src, rx1.at[h, kind], s1_send.at[h, kind], s1_recv.at[h, kind], dev1(h, step))

    def stage2(h, kind):
        base = at1(h, OWN)
        src, step = {
            0: (acc.at[h, base, at2(h, OPP), 0:32], RIGHT),
            1: (acc.at[h, base, at2(h, RIGHT), 32:64], RIGHT),
            2: (acc.at[h, base, at2(h, OPP), 32:64], LEFT),
            3: (acc.at[h, base, at2(h, LEFT), 0:32], LEFT),
            4: (acc.at[h, base, at2(h, RIGHT), 0:32], RIGHT),
            5: (acc.at[h, base, at2(h, LEFT), 32:64], LEFT),
        }[kind]
        return remote(src, rx2.at[h, kind], s2_send.at[h, kind], s2_recv.at[h, kind], dev2(h, step))

    def stage3(h):
        src = acc.at[h, at1(h, OWN), at2(h, OWN), pl.ds((1 - pz) * 32, 32)]
        return remote(src, rx3.at[h], s3_send.at[h], s3_recv.at[h], (slab_at(py, px, 1 - pz), b))

    waited = set()
    group0 = (b % 4) * 16

    def unit(h, step):
        for key in strips_of(h, step):
            if key not in waited:
                waited.add(key)
                strip(*key).wait()
        cols = slice(h * half, (h + 1) * half)
        where = at1(h, step)
        left = pan_v[where] if h == 0 else pan_v[:, where]
        left = left.reshape(256, left.shape[-1])
        right = inc_v[:, :, cols].reshape(left.shape[-1], half)
        product = jnp.dot(left, right, preferred_element_type=F32).reshape(4, 64, half)
        for i in range(4):
            group = group0 + (where * 4 + i if h == 0 else i * 4 + where)
            acc[h, where, i] = product[i] + weight * inc_v[group, :, cols].astype(F32)

    loads[2].wait()
    unit(0, OPP)
    stage1(0, 0).start()
    stage1(0, 2).start()
    loads[3].wait()
    unit(1, OPP)
    stage1(1, 0).start()
    stage1(1, 2).start()
    for h in (0, 1):
        unit(h, RIGHT)
        stage1(h, 1).start()
        unit(h, LEFT)
        stage1(h, 3).start()

    def pass_on1(h):
        stage1(h, 0).wait_recv()
        acc[h, at1(h, RIGHT), 0:2] += rx1[h, 0]
        stage1(h, 4).start()
        stage1(h, 2).wait_recv()
        acc[h, at1(h, LEFT), 2:4] += rx1[h, 2]
        stage1(h, 5).start()

    pass_on1(0)
    pass_on1(1)
    unit(0, OWN)
    unit(1, OWN)

    lane = lax.broadcasted_iota(jnp.int32, (chunk, width), 1)

    def sweep(grid, c, store):
        base = 8 + c * chunk
        for z in range(1, 1 + depth):
            def at(dz, dy):
                return grid[z + dz, base + dy : base + dy + chunk, :]

            ends = at(-1, 0) + at(1, 0)
            diagonal = (at(-1, -1) + at(1, -1)) + (at(-1, 1) + at(1, 1))
            plus = ends + (at(0, -1) + at(0, 1))
            mixed = 0.5 * diagonal + plus
            along = jnp.where(lane == 0, 0.0, pltpu.roll(mixed, 1, 1)) + jnp.where(
                lane == width - 1, 0.0, pltpu.roll(mixed, width - 1, 1)
            )
            center = at(0, 0)
            mass = abs_v[z - 1, c * chunk : (c + 1) * chunk, :]
            rhs = src_v[z - 1, c * chunk : (c + 1) * chunk, :]
            applied = CENTER * center - (diagonal + along) * (1.0 / 6.0) + mass * center
            store(z, c, center + OMEGA * (rhs - applied) / (CENTER + mass))

    def store1(z, c, value):
        grid1[z, 8 + c * chunk : 8 + (c + 1) * chunk, :] = value

    def store2(z, c, value):
        relaxed_ref[z - 1, c * chunk : (c + 1) * chunk, :] = value

    loads[4].wait()
    loads[5].wait()
    place_y(grid0, 0, 0)
    place_y(grid0, 0, 1)
    wait_z(grid0, 0, 0)
    for c in range(CHUNKS):
        if c + 1 < CHUNKS:
            wait_z(grid0, 0, c + 1)
        sweep(grid0, c, store1)
        start_z(grid1, 1, c)
        if c == 0:
            pack_rows(grid1, 1, 0)
            start_y(1, 0)
        if c == CHUNKS - 1:
            pack_rows(grid1, 1, 1)
            start_y(1, 1)

    def finish1(h):
        base = at1(h, OWN)
        for kind in (1, 3, 4, 5):
            stage1(h, kind).wait_recv()
        acc[h, base, 0:2] = acc[h, base, 0:2] + (rx1[h, 4] + rx1[h, 3])
        acc[h, base, 2:4] = acc[h, base, 2:4] + (rx1[h, 1] + rx1[h, 5])
        for kind in (0, 2, 1, 3):
            stage2(h, kind).start()

    def pass_on2(h):
        base = at1(h, OWN)
        stage2(h, 0).wait_recv()
        acc[h, base, at2(h, RIGHT), 0:32] += rx2[h, 0]
        stage2(h, 4).start()
        stage2(h, 2).wait_recv()
        acc[h, base, at2(h, LEFT), 32:64] += rx2[h, 2]
        stage2(h, 5).start()

    def finish2(h):
        base, own = at1(h, OWN), at2(h, OWN)
        for kind in (1, 3, 4, 5):
            stage2(h, kind).wait_recv()
        acc[h, base, own, 0:32] = acc[h, base, own, 0:32] + (rx2[h, 4] + rx2[h, 3])
        acc[h, base, own, 32:64] = acc[h, base, own, 32:64] + (rx2[h, 1] + rx2[h, 5])
        stage3(h).start()

    for k in range(1, NBLK):
        landed_trace(k).wait_recv()
    tmat[...] = jnp.zeros_like(tmat)
    for n in range(NBLK):
        for q in range(4):
            row = trace[n, q : q + 1, :]
            top = row.astype(BF16).astype(F32)
            place = slice((4 * n + q) * 128, (4 * n + q + 1) * 128)
            tmat[0:1, place] = top
            tmat[1:2, place] = row - top

    def square(n, total):
        columns = jnp.transpose(trace[n])
        for q in range(4):
            column = columns[:, q : q + 1]
            for part in range(2):
                wide = inc_v[n * 8 + q * 2 + part].astype(F32) + column[part * 64 : (part + 1) * 64]
                total = total + jnp.sum((wide * wide).reshape(8, 8, 2 * half), axis=0)
        return total

    squares = lax.fori_loop(0, NBLK, square, jnp.zeros((8, 2 * half), F32))
    squares = jnp.sum(squares, axis=0, keepdims=True)
    terms = tmat[...].astype(BF16)
    for y in range(4):
        reach = lax.dot_general(
            terms,
            pan_v[y].reshape(256, pan_v.shape[-1]),
            (((1,), (1,)), ((), ())),
            preferred_element_type=F32,
        )
        reach = reach[0:1] + reach[1:2]
        for m in range(2):
            block = 2 * y + m
            jump = trace[2 * (b % 4) + block // 4, block % 4 : block % 4 + 1, :]
            line = reach[:, m * 128 : (m + 1) * 128] + weight * jump
            msgs[block] = jnp.concatenate(
                [squares[:, q * 128 : (q + 1) * 128] for q in range(4)] + [line, jnp.zeros((3, 128), F32)], axis=0
            )

    def copy_sums(k):
        other = (s + k) % NSLAB
        return remote(msgs.at[other // 4], a2a.at[k], aa_send.at[k], aa_recv.at[k], (other, b))

    def start_sums(k, carry):
        copy_sums(k).start()
        return carry

    lax.fori_loop(1, NSLAB, start_sums, 0)

    finish1(0)
    finish1(1)
    pass_on2(0)
    pass_on2(1)
    finish2(0)
    finish2(1)

    place_y(grid1, 1, 0)
    place_y(grid1, 1, 1)
    wait_z(grid1, 1, 0)
    for c in range(CHUNKS):
        if c + 1 < CHUNKS:
            wait_z(grid1, 1, c + 1)
        sweep(grid1, c, store2)

    def add_sums(k, total):
        copy_sums(k).wait_recv()
        return total + a2a[k]

    total = lax.fori_loop(1, NSLAB, add_sums, msgs[s // 4])
    norms = jnp.concatenate([total[q : q + 1] for q in range(4)], axis=1)
    norms = jnp.sqrt(norms * (1.0 / (NSLAB * NBLK * 512)) + 1e-06)
    pick = lax.broadcasted_iota(jnp.int32, (32, 128), 1) == (s % 4) * 32 + lax.broadcasted_iota(
        jnp.int32, (32, 128), 0
    )
    reach = jnp.sum(jnp.where(pick, total[4:5], 0.0), axis=1, keepdims=True)
    for h in (0, 1):
        stage3(h).wait_recv()
        own = acc[h, at1(h, OWN), at2(h, OWN), pl.ds(pz * 32, 32)] + rx3[h]
        cols = slice(h * half, (h + 1) * half)
        flux_ref[:, cols] = (own + reach) / norms[:, cols]

    def drain_sums(k, carry):
        copy_sums(k).wait_send()
        return carry

    lax.fori_loop(1, NSLAB, drain_sums, 0)
    for h in (0, 1):
        for kind in range(6):
            stage1(h, kind).wait_send()
            stage2(h, kind).wait_send()
        stage3(h).wait_send()
    for k in range(1, NBLK):
        copy_trace(k).wait_send()
    for rnd, grid in ((0, grid0), (1, grid1)):
        for c in range(CHUNKS):
            drain_z(grid, rnd, c)
        for side in (0, 1):
            for slot in range(3):
                halo_y(rnd, side, slot).wait_send()


def per_device(interior, sources, absorption, bem_panel, incident, node_cell, offset):
    depth, rows, width = interior.shape
    nodes, fields = incident.shape
    panel_rows = bem_panel.shape[0]
    half = fields // 2
    anywhere = pl.BlockSpec(memory_space=pl.ANY)
    local = pl.BlockSpec(memory_space=pltpu.VMEM)
    dma = pltpu.SemaphoreType.DMA
    return pl.pallas_call(
        kernel,
        out_shape=(
            jax.ShapeDtypeStruct((depth, rows, width), F32),
            jax.ShapeDtypeStruct((panel_rows // NSLAB, fields), F32),
        ),
        in_specs=[pl.BlockSpec(memory_space=pltpu.SMEM)] + [anywhere] * 6,
        out_specs=(local, local),
        scratch_shapes=[
            pltpu.VMEM((depth + 2, rows + 16, width), F32),
            pltpu.VMEM((depth + 2, rows + 16, width), F32),
            pltpu.VMEM((depth, rows, width), F32),
            pltpu.VMEM((depth, rows, width), F32),
            pltpu.VMEM((nodes // 128, 128), jnp.int32),
            pltpu.VMEM((nodes // 64, 64, fields), BF16),
            pltpu.VMEM((4, 4, 64, nodes), BF16),
            pltpu.VMEM((2, 4, 4, 64, half), F32),
            pltpu.VMEM((2, 6, 2, 64, half), F32),
            pltpu.VMEM((2, 6, 32, half), F32),
            pltpu.VMEM((2, 32, half), F32),
            pltpu.VMEM((2, 2, 8, width), F32),
            pltpu.VMEM((2, 2, 3, 8, width), F32),
            pltpu.VMEM((NBLK, 8, 128), F32),
            pltpu.VMEM((16, nodes), F32),
            pltpu.VMEM((8, 8, 128), F32),
            pltpu.VMEM((NSLAB, 8, 128), F32),
            dma((4, 4)),
            dma((6,)),
            dma((2, 6)),
            dma((2, 6)),
            dma((2, 6)),
            dma((2, 6)),
            dma((2,)),
            dma((2,)),
            dma((2, CHUNKS, 2)),
            dma((2, CHUNKS, 2)),
            dma((2, 2, 3)),
            dma((2, 2, 3)),
            dma((NBLK,)),
            dma((NBLK,)),
            dma((NSLAB,)),
            dma((NSLAB,)),
        ],
        compiler_params=pltpu.CompilerParams(collective_id=0, has_side_effects=True),
    )(
        offset,
        interior,
        sources,
        absorption,
        bem_panel.reshape(4, 4, panel_rows // 16, nodes),
        incident.reshape(nodes // 64, 64, fields),
        node_cell.reshape(nodes // 128, 128),
    )


def solution(mesh):
    in_specs = (
        P("slab", "blk", None),
        P("slab", "blk", None),
        P("slab", "blk", None),
        P("blk", "slab"),
        P("slab", None),
        P("slab"),
        P(),
    )
    out_specs = (P("slab", "blk", None), P(("blk", "slab"), None))
    return jax.shard_map(
        per_device, mesh=mesh, in_specs=in_specs, out_specs=out_specs, check_vma=False
    )
```
